256 devices in a mesh: grp: 4 (over y), col: 64 (over x, z, core).
Axes of the slice: x: 4, y: 4, z: 8, core: 2. Of those that a mesh axis runs over, the one named last changes fastest.
Arguments:
- right_side: float32 [2048, 2048], P('grp', 'col'), may hold values from -6 to 6
- solved_factor: float32 [2048, 49152], P('grp', 'col'), may hold values from -0.02734375 to 0.02734375
- solved_users: float32 [49152, 2048], P('col'), may hold values from -16 to 16
- diag_inverse: float32 [2048, 512], P('grp'), may hold values from -0.25 to 0.25
- coupling: float32 [2048, 1536], P('grp'), may hold values from -0.25 to 0.25
Outputs:
- solution: float32 [2048, 2048], P('grp', 'col')
The draws below stay inside these ranges and needn't reach their ends.
All inputs are finite; a program needn't handle non-finite values.
Results may differ from the reference program's by a relative error of at most 0.0001.
Values sent between devices are 32-bit elements; how exact they have to be, the bound alone decides.
No kernel may reach another device: no remote copies, remote signals or barrier semaphores. Data moves between devices by JAX's collectives and lax.ppermute only.
A program may use at most 64 MiB of HBM per device.

```python
import jax
import jax.numpy as jnp
from jax import lax

ITEMS = 2048
BLOCK = 512
SOLVED = 49152
WINDOW = 2048
N_GRP = 4


def with_spikes(entries, rng, source, target, parts, factor):
    owner, partner = [(jnp.arange(entries.shape[axis_at]) // (entries.shape[axis_at] // parts)).reshape([-1 if axis == axis_at else 1 for axis in range(entries.ndim)]) for axis_at in (source, target)]
    chosen = jax.random.permutation(rng, parts)[partner]
    strong = (owner == chosen) | (owner == (partner + parts // 2) % parts)
    return jnp.where(strong, factor * entries, entries)


def levels(own_key, dims, cuts, low, high):
    level = 1.0
    for axis_at, parts in cuts:
        heights = jax.random.uniform(jax.random.fold_in(jax.random.fold_in(own_key, 6), axis_at), (parts,), jnp.float32, low / len(cuts), high / len(cuts))
        level = level * jnp.repeat(jnp.exp(heights), dims[axis_at] // parts).reshape((-1,) + (1,) * (len(dims) - 1 - axis_at))
    return level


def normal_values(rng, shape, width, reach, split=(), kind=jnp.bfloat16):
    values = jax.random.normal(rng, shape, jnp.float32) * width
    if len(split) > 0:
        values = levels(rng, shape, split, -0.22, 0.18) * values
    return jnp.clip(values, min=-reach, max=reach).astype(kind)


def noise_with(stream_key, extent, scale, reach, cuts, heavy, kind=jnp.bfloat16):
    entries = scale * jax.random.normal(stream_key, extent, jnp.float32)
    if cuts:
        entries = entries * levels(stream_key, extent, cuts, -0.22, 0.18)
    return jnp.clip(with_spikes(entries, jax.random.fold_in(stream_key, 3), *heavy), -reach, reach).astype(kind)


def setup_inputs(seed: int = 0) -> dict:
    arg_keys = jax.random.split(jax.random.key(seed), 6)
    return {
        "right_side": normal_values(arg_keys[0], (WINDOW, ITEMS), 1.0, 6.0, ((0, 4), (1, 64)), jnp.float32),
        "solved_factor": normal_values(arg_keys[1], (WINDOW, SOLVED), SOLVED ** -0.5, 0.02734375, ((0, 4), (1, 64)), jnp.float32),
        "solved_users": noise_with(arg_keys[2], (SOLVED, ITEMS), 1.0, 16.0, ((0, 64),), (0, 1, 64, 4.0), jnp.float32),
        "diag_inverse": normal_values(arg_keys[3], (WINDOW, BLOCK), BLOCK ** -0.5, 0.25, ((0, 4),), jnp.float32),
        "coupling": normal_values(arg_keys[4], (WINDOW, BLOCK * (N_GRP - 1)), BLOCK ** -0.5, 0.25, ((0, 4),), jnp.float32),
    }


highest = lax.Precision.HIGHEST


def product(left, right):
    return jnp.dot(left, right, precision=highest, preferred_element_type=jnp.float32)


def reference(right_side, solved_factor, solved_users, diag_inverse, coupling):
    reduced = right_side - product(solved_factor, solved_users)
    solved_blocks = []
    for group in range(N_GRP):
        rows = slice(group * BLOCK, (group + 1) * BLOCK)
        residue = reduced[rows]
        for earlier in range(group):
            coupling_block = coupling[rows, earlier * BLOCK:(earlier + 1) * BLOCK]
            residue = residue - product(coupling_block, solved_blocks[earlier])
        solved_blocks.append(product(diag_inverse[rows], residue))
    return jnp.concatenate(solved_blocks, axis=0)
```

```python
import functools

import jax
import jax.numpy as jnp
from jax import lax
from jax.experimental import pallas as pl
from jax.experimental.pallas import tpu as pltpu
from jax.sharding import Mesh
from jax.sharding import PartitionSpec as P

COL = ("x", "z", "core")


def shifted(value, axis, by):
    peers = lax.axis_size(axis)
    return lax.ppermute(value, axis, [(i, (i + by) % peers) for i in range(peers)])


def halves(value):
    high = value.astype(jnp.bfloat16)
    return high, (value - high.astype(jnp.float32)).astype(jnp.bfloat16)


def contract(left, right, left_dim, right_dim):
    dims = (((left_dim,), (right_dim,)), ((), ()))
    return lax.dot_general(left, right, dims, preferred_element_type=jnp.float32)


def three_pass(left, right, left_dim, right_dim):
    left_high, left_low = halves(left)
    right_high, right_low = halves(right)
    return contract(left_high, right_high, left_dim, right_dim) + (
        contract(left_high, right_low, left_dim, right_dim)
        + contract(left_low, right_high, left_dim, right_dim)
    )


def product_body(n_z, n_core, place, users, factor, own_a, own_b, sent_a, sent_b):
    z, core = place[1], place[2]
    items, rows = users.shape[1], factor.shape[0]
    share = items // (n_z * n_core)
    total = three_pass(users[...], factor[...], 0, 1).reshape(n_z, n_core, share, rows)

    def keep(mine):
        for k in range(n_z):
            ahead = lax.rem(k - z + n_z, n_z)
            own, sent = total[k, mine], total[k, 1 - mine]
            own_a[0, ahead] = own[:, : rows // 2]
            own_b[ahead, 0] = own[:, rows // 2 :]
            sent_a[0, ahead] = sent[:, : rows // 2]
            sent_b[ahead, 0] = sent[:, rows // 2 :]

    pl.when(core == 0)(lambda: keep(0))
    pl.when(core == 1)(lambda: keep(1))


def product(place, users, factor, n_x, n_z, n_core):
    depth, items = users.shape
    rows = factor.shape[0]
    chunk, share = items // n_x, items // (n_x * n_z * n_core)
    by_x = pl.BlockSpec((1, n_z, share, rows // 2), lambda i, s: (i, 0, 0, 0))
    by_z = pl.BlockSpec((n_z, 1, share, rows // 2), lambda i, s: (0, i, 0, 0))
    shape_a = jax.ShapeDtypeStruct((n_x, n_z, share, rows // 2), jnp.float32)
    shape_b = jax.ShapeDtypeStruct((n_z, n_x, share, rows // 2), jnp.float32)
    return pl.pallas_call(
        functools.partial(product_body, n_z, n_core),
        grid_spec=pltpu.PrefetchScalarGridSpec(
            num_scalar_prefetch=1,
            grid=(n_x,),
            in_specs=[
                pl.BlockSpec((depth, chunk), lambda i, s: (0, lax.rem(s[0] + i, n_x))),
                pl.BlockSpec((rows, depth), lambda i, s: (0, 0)),
            ],
            out_specs=[by_x, by_z, by_x, by_z],
        ),
        out_shape=[shape_a, shape_b, shape_a, shape_b],
        compiler_params=pltpu.CompilerParams(vmem_limit_bytes=40 << 20),
    )(place, users, factor)


def ring_reduced(blocks, axis):
    blocks = list(blocks)
    peers = len(blocks)
    far = peers // 2
    cut = blocks[far].shape[0] // 2
    up = shifted(blocks[far][:cut], axis, 1)
    down = shifted(blocks[far][cut:], axis, -1)
    ahead, behind = far - 1, far + 1
    first, second = blocks[ahead], blocks[behind]
    blocks[ahead] = jnp.concatenate([first[:cut] + up, first[cut:]])
    blocks[behind] = jnp.concatenate([second[:cut], second[cut:] + down])
    for step in range(far - 1, 0, -1):
        up = shifted(blocks[step], axis, 1)
        down = shifted(blocks[peers - step], axis, -1)
        if step > 1:
            blocks[step - 1] = blocks[step - 1] + up
            blocks[peers - step + 1] = blocks[peers - step + 1] + down
    return blocks[0] + up + down


def direct_reduced(blocks, axis):
    peers = len(blocks)
    order = sorted(range(1, peers), key=lambda o: -min(o, peers - o))
    parts = [shifted(blocks[o], axis, o) for o in order]
    return functools.reduce(lambda a, b: a + b, parts, blocks[0])


def apply_rows(vectors, matrix):
    return jnp.dot(vectors, matrix.T, precision="highest", preferred_element_type=jnp.float32)


def chain(residue, diag_inverse, coupled):
    position = lax.axis_index("grp")
    groups = lax.axis_size("grp")

    def only(where, value):
        return jnp.where(where, value, jnp.zeros_like(value))

    result = apply_rows(residue, diag_inverse)
    later = []
    for step in range(groups - 1):
        near = shifted(result, "grp", 1)
        far = [(by, shifted(result, "grp", by)) for by in range(2, groups - step)]
        change = apply_rows(only(position == step + 1, near), coupled[step])
        for other, value in later:
            change = change + apply_rows(value, coupled[other])
        result = result - change
        later = [
            (step, functools.reduce(lambda a, b: a + b, [only(position == step + by, v) for by, v in far]))
        ] if far else []
    return result


def on_device(right_side, solved_factor, solved_users, diag_inverse, coupling):
    n_x, n_z, n_core = (lax.axis_size(a) for a in COL)
    place = jnp.stack([lax.axis_index(a) for a in COL]).astype(jnp.int32)
    own_a, own_b, sent_a, sent_b = product(place, solved_users, solved_factor, n_x, n_z, n_core)
    block = diag_inverse.shape[0]
    coupled = [
        jnp.dot(
            diag_inverse,
            coupling[:, h * block : (h + 1) * block],
            precision="highest",
            preferred_element_type=jnp.float32,
        )
        for h in range(coupling.shape[1] // block)
    ]
    sum_b = own_b + shifted(sent_b, "core", 1)
    sum_a = [None] * n_x
    for o in sorted(range(n_x), key=lambda o: -min(o, n_x - o)):
        sum_a[o] = own_a[o] + shifted(sent_a[o], "core", 1)
    part_b = ring_reduced([sum_b[o] for o in range(n_z)], "z")
    part_a = ring_reduced(sum_a, "x")
    share_a = direct_reduced([part_a[o] for o in range(n_z)], "z")
    share_b = direct_reduced([part_b[o] for o in range(n_x)], "x")
    residue = right_side.T - jnp.concatenate([share_a, share_b], axis=1)
    return chain(residue, diag_inverse, coupled).T


def solution(mesh):
    torus = Mesh(mesh.devices.reshape(mesh.shape["grp"], 4, 8, 2), ("grp",) + COL)
    placed = (P("grp", COL), P("grp", COL), P(COL, None), P("grp", None), P("grp", None))
    return jax.shard_map(
        on_device, mesh=torus, in_specs=placed, out_specs=P("grp", COL), check_vma=False
    )
```

```python
import functools

import jax
import jax.numpy as jnp
from jax import lax
from jax.experimental import pallas as pl
from jax.experimental.pallas import tpu as pltpu
from jax.sharding import Mesh
from jax.sharding import PartitionSpec as P

COL = ("x", "z", "core")


def shifted(value, axis, by):
    peers = lax.axis_size(axis)
    return lax.ppermute(value, axis, [(i, (i + by) % peers) for i in range(peers)])


def summed_at_owner(blocks, axis):
    return jnp.sum(lax.all_to_all(blocks, axis, 0, 0, tiled=True), axis=0)


def halves(value):
    high = value.astype(jnp.bfloat16)
    return high, (value - high.astype(jnp.float32)).astype(jnp.bfloat16)


def contract(left, right, left_dim, right_dim):
    dims = (((left_dim,), (right_dim,)), ((), ()))
    return lax.dot_general(left, right, dims, preferred_element_type=jnp.float32)


def three_pass(left, right, left_dim, right_dim):
    left_high, left_low = halves(left)
    right_high, right_low = halves(right)
    return contract(left_high, right_high, left_dim, right_dim) + (
        contract(left_high, right_low, left_dim, right_dim)
        + contract(left_low, right_high, left_dim, right_dim)
    )


def ring_order(peers):
    return sorted(range(peers), key=lambda o: (-min(o, peers - o), o))


def product_body(n_z, n_core, split, place, users, factor, far_own, own_a, own_b, far_sent, sent_a, sent_b):
    core, step = place[0], pl.program_id(0)
    items, rows = users.shape[1], factor.shape[0]
    share = items // (n_z * n_core)
    total = three_pass(users[...], factor[...], 0, 1).reshape(n_z, n_core, share, rows)

    def keep(mine):
        own, sent = total[:, mine], total[:, 1 - mine]
        own_b[:, 0] = own[..., split:]
        sent_b[:, 0] = sent[..., split:]

        @pl.when(step == 0)
        def _():
            far_own[...] = own[..., :split]
            far_sent[...] = sent[..., :split]

        @pl.when(step > 0)
        def _():
            own_a[0] = own[..., :split]
            sent_a[0] = sent[..., :split]

    pl.when(core == 0)(lambda: keep(0))
    pl.when(core == 1)(lambda: keep(1))


def product(place, users, factor, n_x, n_z, n_core, split):
    depth, items = users.shape
    rows = factor.shape[0]
    chunk, share = items // n_x, items // (n_x * n_z * n_core)
    specs = [
        pl.BlockSpec((n_z, share, split), lambda i, s: (0, 0, 0)),
        pl.BlockSpec((1, n_z, share, split), lambda i, s: (lax.max(i - 1, 0), 0, 0, 0)),
        pl.BlockSpec((n_z, 1, share, rows - split), lambda i, s: (0, s[1 + i], 0, 0)),
    ]
    shapes = [
        jax.ShapeDtypeStruct((n_z, share, split), jnp.float32),
        jax.ShapeDtypeStruct((n_x - 1, n_z, share, split), jnp.float32),
        jax.ShapeDtypeStruct((n_z, n_x, share, rows - split), jnp.float32),
    ]
    return pl.pallas_call(
        functools.partial(product_body, n_z, n_core, split),
        grid_spec=pltpu.PrefetchScalarGridSpec(
            num_scalar_prefetch=1,
            grid=(n_x,),
            in_specs=[
                pl.BlockSpec((depth, chunk), lambda i, s: (0, s[1 + i])),
                pl.BlockSpec((rows, depth), lambda i, s: (0, 0)),
            ],
            out_specs=specs * 2,
        ),
        out_shape=shapes * 2,
        compiler_params=pltpu.CompilerParams(vmem_limit_bytes=56 << 20),
    )(place, users, factor)


def weights_body(diag, coupling, high, low):
    step = pl.program_id(0)

    def keep(value):
        high[0], low[0] = halves(value)

    pl.when(step == 0)(lambda: keep(diag[...].T))
    pl.when(step > 0)(lambda: keep(-three_pass(coupling[...], diag[...], 0, 1)))


def hop_weights(diag, coupling):
    block = diag.shape[0]
    count = 1 + coupling.shape[1] // block
    shape = jax.ShapeDtypeStruct((count, block, block), jnp.bfloat16)
    return pl.pallas_call(
        weights_body,
        grid=(count,),
        in_specs=[
            pl.BlockSpec((block, block), lambda i: (0, 0)),
            pl.BlockSpec((block, block), lambda i: (0, lax.max(i - 1, 0))),
        ],
        out_specs=[pl.BlockSpec((1, block, block), lambda i: (i, 0, 0))] * 2,
        out_shape=[shape] * 2,
        compiler_params=pltpu.CompilerParams(vmem_limit_bytes=24 << 20),
    )(diag, coupling)


def apply_body(wanted, place, *refs):
    *values, base, high, low, out = refs
    total = jnp.zeros_like(base)
    for group, value in zip(wanted, values):
        total = total + (value[...] if group is None else jnp.where(place[0] == group, value[...], 0.0))
    value_high, value_low = halves(total)
    count = value_high.shape[0]
    both = contract(jnp.concatenate([value_high, value_low]), high[0], 1, 0)
    out[...] = base[...] + (both[:count] + both[count:] + contract(value_high, low[0], 1, 0))


def applied(position, base, values, weights, index):
    whole = pl.BlockSpec(base.shape, lambda i, s: (0, 0))
    block = weights[0].shape[1]
    weight = pl.BlockSpec((1, block, block), lambda i, s: (index, 0, 0))
    return pl.pallas_call(
        functools.partial(apply_body, [group for group, _ in values]),
        grid_spec=pltpu.PrefetchScalarGridSpec(
            num_scalar_prefetch=1,
            grid=(1,),
            in_specs=[whole] * (len(values) + 1) + [weight] * 2,
            out_specs=whole,
        ),
        out_shape=jax.ShapeDtypeStruct(base.shape, jnp.float32),
        compiler_params=pltpu.CompilerParams(vmem_limit_bytes=8 << 20),
    )(position, *[value for _, value in values], base, *weights)


def chain(position, residue, weights):
    groups = lax.axis_size("grp")
    result = applied(position, jnp.zeros_like(residue), [(None, residue)], weights, 0)
    later = []
    for step in range(groups - 1):
        near = shifted(result, "grp", 1)
        far = [(step + by, shifted(result, "grp", by)) for by in range(2, groups - step)]
        if later:
            result = applied(position, result, later, weights, step)
        result = applied(position, result, [(step + 1, near)], weights, step + 1)
        later = far
    return result


def ring_reduced(far, near, axis):
    cut = far.shape[0] // 2
    up = shifted(far[:cut], axis, 1)
    down = shifted(far[cut:], axis, -1)
    up = shifted(jnp.concatenate([near[0, :cut] + up, near[0, cut:]]), axis, 1)
    down = shifted(jnp.concatenate([near[1, :cut], near[1, cut:] + down]), axis, -1)
    return near[2] + up + down


def on_device(right_side, solved_factor, solved_users, diag_inverse, coupling):
    n_x, n_z, n_core = (lax.axis_size(a) for a in COL)
    x, core = lax.axis_index("x"), lax.axis_index("core")
    place = jnp.stack([core] + [(x + o) % n_x for o in ring_order(n_x)]).astype(jnp.int32)
    position = lax.axis_index("grp").reshape(1).astype(jnp.int32)
    rows = solved_factor.shape[0]
    far_own, own_a, own_b, far_sent, sent_a, sent_b = product(
        place, solved_users, solved_factor, n_x, n_z, n_core, rows * 3 // 4
    )
    weights = hop_weights(diag_inverse, coupling)
    sum_b = own_b + shifted(sent_b, "core", 1)
    far_a = far_own + shifted(far_sent, "core", 1)
    near_a = own_a + shifted(sent_a, "core", 1)
    part_b = summed_at_owner(sum_b, "z")
    part_a = ring_reduced(far_a, near_a, "x")
    share_b = summed_at_owner(part_b, "x")
    share_a = summed_at_owner(part_a, "z")
    residue = right_side.T - jnp.concatenate([share_a, share_b], axis=1)
    return chain(position, residue, weights).T


def solution(mesh):
    torus = Mesh(mesh.devices.reshape(mesh.shape["grp"], 4, 8, 2), ("grp",) + COL)
    placed = (P("grp", COL), P("grp", COL), P(COL, None), P("grp", None), P("grp", None))
    return jax.shard_map(
        on_device, mesh=torus, in_specs=placed, out_specs=P("grp", COL), check_vma=False
    )
```

```python
import functools

import jax
import jax.numpy as jnp
from jax import lax
from jax.experimental import pallas as pl
from jax.experimental.pallas import tpu as pltpu
from jax.sharding import Mesh
from jax.sharding import PartitionSpec as P

COL = ("x", "z", "core")


def shifted(value, axis, by):
    peers = lax.axis_size(axis)
    return lax.ppermute(value, axis, [(i, (i + by) % peers) for i in range(peers)])


def summed_at_owner(blocks, axis):
    return jnp.sum(lax.all_to_all(blocks, axis, 0, 0, tiled=True), axis=0)


def in_hbm(value):
    return pltpu.with_memory_space_constraint(value, pltpu.HBM)


def halves(value):
    high = value.astype(jnp.bfloat16)
    return high, (value - high.astype(jnp.float32)).astype(jnp.bfloat16)


def contract(left, right, left_dim, right_dim):
    dims = (((left_dim,), (right_dim,)), ((), ()))
    return lax.dot_general(left, right, dims, preferred_element_type=jnp.float32)


def three_pass(left, right, left_dim, right_dim):
    left_high, left_low = halves(left)
    right_high, right_low = halves(right)
    return contract(left_high, right_high, left_dim, right_dim) + (
        contract(left_high, right_low, left_dim, right_dim)
        + contract(left_low, right_high, left_dim, right_dim)
    )


def ring_order(peers):
    return sorted(range(peers), key=lambda o: (-min(o, peers - o), o))


def product_body(n_z, n_core, place, users, factor, own_out, sent_out):
    items, rows = users.shape[1], factor.shape[0]
    share = items // (n_z * n_core)
    total = three_pass(users[...], factor[...], 0, 1).reshape(n_z, n_core, share, rows)

    def keep(mine):
        own_out[0] = total[:, mine]
        sent_out[0] = total[:, 1 - mine]

    pl.when(place[0] == 0)(lambda: keep(0))
    pl.when(place[0] == 1)(lambda: keep(1))


def product(place, first, count, users, factor, sizes):
    n_x, n_z, n_core = sizes
    depth, items = users.shape
    rows = factor.shape[0]
    chunk, share = items // n_x, items // (n_x * n_z * n_core)
    return pl.pallas_call(
        functools.partial(product_body, n_z, n_core),
        grid_spec=pltpu.PrefetchScalarGridSpec(
            num_scalar_prefetch=1,
            grid=(count,),
            in_specs=[
                pl.BlockSpec((depth, chunk), lambda i, s: (0, s[1 + first + i])),
                pl.BlockSpec((rows, depth), lambda i, s: (0, 0)),
            ],
            out_specs=[pl.BlockSpec((1, n_z, share, rows), lambda i, s: (i, 0, 0, 0))] * 2,
        ),
        out_shape=[jax.ShapeDtypeStruct((count, n_z, share, rows), jnp.float32)] * 2,
        compiler_params=pltpu.CompilerParams(vmem_limit_bytes=24 << 20),
    )(place, users, factor)


def weights_body(diag, coupling, high, low):
    step = pl.program_id(0)

    def keep(value):
        high[0], low[0] = halves(value)

    pl.when(step == 0)(lambda: keep(diag[...].T))
    pl.when(step > 0)(lambda: keep(-three_pass(coupling[...], diag[...], 0, 1)))


def hop_weights(diag, coupling):
    block = diag.shape[0]
    count = 1 + coupling.shape[1] // block
    shape = jax.ShapeDtypeStruct((count, block, block), jnp.bfloat16)
    return pl.pallas_call(
        weights_body,
        grid=(count,),
        in_specs=[
            pl.BlockSpec((block, block), lambda i: (0, 0)),
            pl.BlockSpec((block, block), lambda i: (0, lax.max(i - 1, 0))),
        ],
        out_specs=[pl.BlockSpec((1, block, block), lambda i: (i, 0, 0))] * 2,
        out_shape=[shape] * 2,
        compiler_params=pltpu.CompilerParams(vmem_limit_bytes=24 << 20),
    )(diag, coupling)


def apply_body(wanted, place, *refs):
    *values, base, high, low, out = refs
    total = jnp.zeros_like(base)
    for group, value in zip(wanted, values):
        total = total + (value[...] if group is None else jnp.where(place[0] == group, value[...], 0.0))
    value_high, value_low = halves(total)
    count = value_high.shape[0]
    both = contract(jnp.concatenate([value_high, value_low]), high[0], 1, 0)
    out[...] = base[...] + (both[:count] + both[count:] + contract(value_high, low[0], 1, 0))


def applied(position, base, values, weights, index):
    whole = pl.BlockSpec(base.shape, lambda i, s: (0, 0))
    block = weights[0].shape[1]
    weight = pl.BlockSpec((1, block, block), lambda i, s: (index, 0, 0))
    return pl.pallas_call(
        functools.partial(apply_body, [group for group, _ in values]),
        grid_spec=pltpu.PrefetchScalarGridSpec(
            num_scalar_prefetch=1,
            grid=(1,),
            in_specs=[whole] * (len(values) + 1) + [weight] * 2,
            out_specs=whole,
        ),
        out_shape=jax.ShapeDtypeStruct(base.shape, jnp.float32),
        compiler_params=pltpu.CompilerParams(vmem_limit_bytes=8 << 20),
    )(position, *[value for _, value in values], base, *weights)


def chain(position, residue, weights):
    groups = lax.axis_size("grp")
    result = applied(position, jnp.zeros_like(residue), [(None, residue)], weights, 0)
    later = []
    for step in range(groups - 1):
        near = shifted(result, "grp", 1)
        far = [(step + by, shifted(result, "grp", by)) for by in range(2, groups - step)]
        if later:
            result = applied(position, result, later, weights, step)
        result = applied(position, result, [(step + 1, near)], weights, step + 1)
        later = far
    return result


def on_device(right_side, solved_factor, solved_users, diag_inverse, coupling):
    sizes = tuple(lax.axis_size(a) for a in COL)
    x, core = lax.axis_index("x"), lax.axis_index("core")
    place = jnp.stack([core] + [(x + o) % sizes[0] for o in ring_order(sizes[0])]).astype(jnp.int32)
    position = lax.axis_index("grp").reshape(1).astype(jnp.int32)
    users, factor = in_hbm(solved_users), in_hbm(solved_factor)

    def part(first, count, place):
        own, sent = product(place, first, count, users, factor, sizes)
        place, sent = lax.optimization_barrier((place, sent))
        return own, shifted(sent, "core", 1), place

    far_own, far_other, place = part(0, 1, place)
    near_own, near_other, place = part(1, 2, place)
    far = (far_own + far_other)[0]
    place, far = lax.optimization_barrier((place, far))
    cut = far.shape[0] // 2
    up = shifted(far[:cut], "x", 1)
    down = shifted(far[cut:], "x", -1)
    home_own, home_other, _ = part(3, 1, place)
    weights = [in_hbm(half) for half in hop_weights(diag_inverse, coupling)]
    ahead, behind = near_own[0] + near_other[0], near_own[1] + near_other[1]
    up = shifted(jnp.concatenate([ahead[:cut] + up, ahead[cut:]]), "x", 1)
    down = shifted(jnp.concatenate([behind[:cut], behind[cut:] + down]), "x", -1)
    along_z = home_own[0] + home_other[0] + up + down
    residue = right_side.T - summed_at_owner(along_z, "z")
    return chain(position, residue, weights).T


def solution(mesh):
    torus = Mesh(mesh.devices.reshape(mesh.shape["grp"], 4, 8, 2), ("grp",) + COL)
    placed = (P("grp", COL), P("grp", COL), P(COL, None), P("grp", None), P("grp", None))
    return jax.shard_map(
        on_device, mesh=torus, in_specs=placed, out_specs=P("grp", COL), check_vma=False
    )
```

```python
import functools

import jax
import jax.numpy as jnp
from jax import lax
from jax.experimental import pallas as pl
from jax.experimental.pallas import tpu as pltpu
from jax.sharding import Mesh
from jax.sharding import PartitionSpec as P

COL = ("x", "z", "core")


def shifted(value, axis, by):
    peers = lax.axis_size(axis)
    return lax.ppermute(value, axis, [(i, (i + by) % peers) for i in range(peers)])


def in_hbm(value):
    return pltpu.with_memory_space_constraint(value, pltpu.HBM)


def halves(value):
    high = value.astype(jnp.bfloat16)
    return high, (value - high.astype(jnp.float32)).astype(jnp.bfloat16)


def contract(left, right, left_dim, right_dim):
    dims = (((left_dim,), (right_dim,)), ((), ()))
    return lax.dot_general(left, right, dims, preferred_element_type=jnp.float32)


def three_pass(left, right, left_dim, right_dim):
    left_high, left_low = halves(left)
    right_high, right_low = halves(right)
    return contract(left_high, right_high, left_dim, right_dim) + (
        contract(left_high, right_low, left_dim, right_dim)
        + contract(left_low, right_high, left_dim, right_dim)
    )


def ring_order(peers):
    return sorted(range(peers), key=lambda o: (-min(o, peers - o), o))


def product_body(n_z, n_core, place, users, factor, far_own, own, far_sent, sent):
    items, rows = users.shape[1], factor.shape[0]
    share = items // (n_z * n_core)
    total = three_pass(users[...], factor[...], 0, 1).reshape(n_z, n_core, share, rows)

    def keep(mine, kept, given):
        for k in range(n_z):
            ahead = lax.rem(k - place[1] + n_z, n_z)
            kept[ahead] = total[k, mine]
            given[ahead] = total[k, 1 - mine]

    for mine in range(2):
        for first in (True, False):
            kept, given = (far_own, far_sent) if first else (own.at[0], sent.at[0])
            chosen = (place[0] == mine) & ((pl.program_id(0) == 0) == first)
            pl.when(chosen)(functools.partial(keep, mine, kept, given))


def product(place, users, factor, sizes):
    n_x, n_z, n_core = sizes
    depth, items = users.shape
    rows = factor.shape[0]
    chunk, share = items // n_x, items // (n_x * n_z * n_core)
    specs = [
        pl.BlockSpec((n_z, share, rows), lambda i, s: (0, 0, 0)),
        pl.BlockSpec((1, n_z, share, rows), lambda i, s: (lax.max(i - 1, 0), 0, 0, 0)),
    ]
    shapes = [
        jax.ShapeDtypeStruct((n_z, share, rows), jnp.float32),
        jax.ShapeDtypeStruct((n_x - 1, n_z, share, rows), jnp.float32),
    ]
    return pl.pallas_call(
        functools.partial(product_body, n_z, n_core),
        grid_spec=pltpu.PrefetchScalarGridSpec(
            num_scalar_prefetch=1,
            grid=(n_x,),
            in_specs=[
                pl.BlockSpec((depth, chunk), lambda i, s: (0, s[2 + i])),
                pl.BlockSpec((rows, depth), lambda i, s: (0, 0)),
            ],
            out_specs=specs * 2,
        ),
        out_shape=shapes * 2,
        cost_estimate=pl.CostEstimate(
            flops=6 * items * rows * depth,
            transcendentals=0,
            bytes_accessed=4 * (items + rows) * depth + 4 * items * rows,
        ),
        compiler_params=pltpu.CompilerParams(vmem_limit_bytes=24 << 20),
    )(place, users, factor)


def weights_body(diag, coupling, high, low):
    step = pl.program_id(0)

    def keep(value):
        high[0], low[0] = halves(value)

    pl.when(step == 0)(lambda: keep(diag[...].T))
    pl.when(step > 0)(lambda: keep(-three_pass(coupling[...], diag[...], 0, 1)))


def hop_weights(diag, coupling):
    block = diag.shape[0]
    count = 1 + coupling.shape[1] // block
    shape = jax.ShapeDtypeStruct((count, block, block), jnp.bfloat16)
    return pl.pallas_call(
        weights_body,
        grid=(count,),
        in_specs=[
            pl.BlockSpec((block, block), lambda i: (0, 0)),
            pl.BlockSpec((block, block), lambda i: (0, lax.max(i - 1, 0))),
        ],
        out_specs=[pl.BlockSpec((1, block, block), lambda i: (i, 0, 0))] * 2,
        out_shape=[shape] * 2,
        cost_estimate=pl.CostEstimate(
            flops=6 * (count - 1) * block**3, transcendentals=0, bytes_accessed=8 * count * block**2
        ),
        compiler_params=pltpu.CompilerParams(vmem_limit_bytes=24 << 20),
    )(diag, coupling)


def apply_body(wanted, place, *refs):
    *values, base, high, low, out = refs
    total = jnp.zeros_like(base)
    for group, value in zip(wanted, values):
        total = total + (value[...] if group is None else jnp.where(place[0] == group, value[...], 0.0))
    value_high, value_low = halves(total)
    count = value_high.shape[0]
    both = contract(jnp.concatenate([value_high, value_low]), high[0], 1, 0)
    out[...] = base[...] + (both[:count] + both[count:] + contract(value_high, low[0], 1, 0))


def applied(position, base, values, weights, index):
    whole = pl.BlockSpec(base.shape, lambda i, s: (0, 0))
    block = weights[0].shape[1]
    weight = pl.BlockSpec((1, block, block), lambda i, s: (index, 0, 0))
    return pl.pallas_call(
        functools.partial(apply_body, [group for group, _ in values]),
        grid_spec=pltpu.PrefetchScalarGridSpec(
            num_scalar_prefetch=1,
            grid=(1,),
            in_specs=[whole] * (len(values) + 1) + [weight] * 2,
            out_specs=whole,
        ),
        out_shape=jax.ShapeDtypeStruct(base.shape, jnp.float32),
        compiler_params=pltpu.CompilerParams(vmem_limit_bytes=8 << 20),
    )(position, *[value for _, value in values], base, *weights)


def chain(position, residue, weights):
    groups = lax.axis_size("grp")
    result = applied(position, jnp.zeros_like(residue), [(None, residue)], weights, 0)
    later = []
    for step in range(groups - 1):
        near = shifted(result, "grp", 1)
        far = [(step + by, shifted(result, "grp", by)) for by in range(2, groups - step)]
        if later:
            result = applied(position, result, later, weights, step)
        result = applied(position, result, [(step + 1, near)], weights, step + 1)
        later = far
    return result


def reduced_over_z(blocks):
    share = blocks.shape[1]
    half = share // 2
    rows = blocks.reshape(-1, blocks.shape[2])
    middle = 4 * share + half
    up = shifted(rows[3 * share : middle], "z", 2)
    down = shifted(rows[middle : 6 * share], "z", -2)
    far_up = jnp.concatenate([blocks[2, :half] + up[share:], blocks[2, half:]])
    far_down = jnp.concatenate([blocks[6, :half], blocks[6, half:] + down[:half]])
    arrived = [
        shifted(far_up, "z", 2),
        shifted(far_down, "z", -2),
        shifted(blocks[1] + up[:share], "z", 1),
        shifted(blocks[7] + down[half:], "z", -1),
    ]
    return functools.reduce(lambda a, b: a + b, arrived, blocks[0])


def on_device(right_side, solved_factor, solved_users, diag_inverse, coupling):
    sizes = tuple(lax.axis_size(a) for a in COL)
    x, z, core = (lax.axis_index(a) for a in COL)
    place = [core, z] + [(x + o) % sizes[0] for o in ring_order(sizes[0])]
    place = jnp.stack(place).astype(jnp.int32)
    position = lax.axis_index("grp").reshape(1).astype(jnp.int32)
    users, factor = in_hbm(solved_users), in_hbm(solved_factor)

    far_own, own, far_sent, sent = product(place, users, factor, sizes)
    far_other = shifted(far_sent, "core", 1)
    sent, far_other = lax.optimization_barrier((sent, far_other))
    far = far_own + far_other
    near = own + shifted(sent, "core", 1)
    cut = far.shape[0] // 2
    up = shifted(far[:cut], "x", 1)
    down = shifted(far[cut:], "x", -1)
    up = shifted(jnp.concatenate([near[0, :cut] + up, near[0, cut:]]), "x", 1)
    down = shifted(jnp.concatenate([near[1, :cut], near[1, cut:] + down]), "x", -1)
    weights = hop_weights(diag_inverse, coupling)
    home, weights = lax.optimization_barrier((near[2], weights))
    along_z = home + up + down
    residue = right_side.T - reduced_over_z(along_z)
    return chain(position, residue, weights).T


def solution(mesh):
    torus = Mesh(mesh.devices.reshape(mesh.shape["grp"], 4, 8, 2), ("grp",) + COL)
    placed = (P("grp", COL), P("grp", COL), P(COL, None), P("grp", None), P("grp", None))
    return jax.shard_map(
        on_device, mesh=torus, in_specs=placed, out_specs=P("grp", COL), check_vma=False
    )
```

```python
import functools

import jax
import jax.numpy as jnp
from jax import lax
from jax.experimental import pallas as pl
from jax.experimental.pallas import tpu as pltpu
from jax.sharding import Mesh
from jax.sharding import PartitionSpec as P

COL = ("x", "z", "core")


def shifted(value, axis, by):
    peers = lax.axis_size(axis)
    return lax.ppermute(value, axis, [(i, (i + by) % peers) for i in range(peers)])


def in_hbm(value):
    return pltpu.with_memory_space_constraint(value, pltpu.HBM)


def halves(value):
    high = value.astype(jnp.bfloat16)
    return high, (value - high.astype(jnp.float32)).astype(jnp.bfloat16)


def contract(left, right, left_dim, right_dim):
    dims = (((left_dim,), (right_dim,)), ((), ()))
    return lax.dot_general(left, right, dims, preferred_element_type=jnp.float32)


def three_pass(left, right, left_dim, right_dim):
    left_high, left_low = halves(left)
    right_high, right_low = halves(right)
    return contract(left_high, right_high, left_dim, right_dim) + (
        contract(left_high, right_low, left_dim, right_dim)
        + contract(left_low, right_high, left_dim, right_dim)
    )


def ring_order(peers):
    return sorted(range(peers), key=lambda o: (-min(o, peers - o), o))


def product_body(n_z, n_core, place, users, factor, own, sent):
    items, rows = users.shape[1], factor.shape[0]
    share = items // (n_z * n_core)
    total = three_pass(users[...], factor[...], 0, 1).reshape(n_z, n_core, share, rows)

    def keep(mine):
        for k in range(n_z):
            ahead = lax.rem(k - place[1] + n_z, n_z)
            own[0, ahead] = total[k, mine]
            sent[0, ahead] = total[k, 1 - mine]

    pl.when(place[0] == 0)(lambda: keep(0))
    pl.when(place[0] == 1)(lambda: keep(1))


def product(place, first, count, users, factor, sizes):
    n_x, n_z, n_core = sizes
    depth, items = users.shape
    rows = factor.shape[0]
    chunk, share = items // n_x, items // (n_x * n_z * n_core)
    return pl.pallas_call(
        functools.partial(product_body, n_z, n_core),
        grid_spec=pltpu.PrefetchScalarGridSpec(
            num_scalar_prefetch=1,
            grid=(count,),
            in_specs=[
                pl.BlockSpec((depth, chunk), lambda i, s: (0, s[2 + first + i])),
                pl.BlockSpec((rows, depth), lambda i, s: (0, 0)),
            ],
            out_specs=[pl.BlockSpec((1, n_z, share, rows), lambda i, s: (i, 0, 0, 0))] * 2,
        ),
        out_shape=[jax.ShapeDtypeStruct((count, n_z, share, rows), jnp.float32)] * 2,
        cost_estimate=pl.CostEstimate(
            flops=6 * count * chunk * rows * depth,
            transcendentals=0,
            bytes_accessed=4 * (count * chunk + rows) * depth + 4 * count * chunk * rows,
        ),
        compiler_params=pltpu.CompilerParams(vmem_limit_bytes=24 << 20),
    )(place, users, factor)


def weights_body(diag, coupling, *outs):
    block = diag.shape[0]
    outs[0][...], outs[1][...] = halves(diag[...].T)
    for h in range(coupling.shape[1] // block):
        value = -three_pass(coupling[:, h * block : (h + 1) * block], diag[...], 0, 1)
        outs[2 + 2 * h][...], outs[3 + 2 * h][...] = halves(value)


def hop_weights(diag, coupling):
    block = diag.shape[0]
    count = 1 + coupling.shape[1] // block
    outs = pl.pallas_call(
        weights_body,
        out_shape=[jax.ShapeDtypeStruct((block, block), jnp.bfloat16)] * (2 * count),
        cost_estimate=pl.CostEstimate(
            flops=6 * (count - 1) * block**3, transcendentals=0, bytes_accessed=8 * count * block**2
        ),
        compiler_params=pltpu.CompilerParams(vmem_limit_bytes=24 << 20),
    )(diag, coupling)
    return [tuple(outs[2 * k : 2 * k + 2]) for k in range(count)]


def apply_body(group, count, place, *refs):
    values, weights, (base, out) = refs[:count], refs[count:-2], refs[-2:]
    total = base[...]
    for k, ref in enumerate(values):
        value = ref[...]
        if group is not None:
            value = jnp.where(place[0] == group, value, 0.0)
        high, low = halves(value)
        both = contract(jnp.concatenate([high, low]), weights[2 * k][...], 1, 0)
        change = both[: high.shape[0]] + both[high.shape[0] :]
        total = total + (change + contract(high, weights[2 * k + 1][...], 1, 0))
    out[...] = total


def applied(position, group, base, terms):
    def rows_at(at):
        return pl.BlockSpec(base.shape, lambda i, s: (at, 0))

    weights = [half for _, _, weight in terms for half in weight]
    return pl.pallas_call(
        functools.partial(apply_body, group, len(terms)),
        grid_spec=pltpu.PrefetchScalarGridSpec(
            num_scalar_prefetch=1,
            grid=(1,),
            in_specs=[rows_at(at) for _, at, _ in terms]
            + [pl.BlockSpec(half.shape, lambda i, s: (0, 0)) for half in weights]
            + [rows_at(0)],
            out_specs=rows_at(0),
        ),
        out_shape=jax.ShapeDtypeStruct(base.shape, jnp.float32),
        compiler_params=pltpu.CompilerParams(vmem_limit_bytes=8 << 20),
    )(position, *[value for value, _, _ in terms], *weights, base)


def chain(position, residue, weights):
    first = applied(position, None, jnp.zeros_like(residue), [(residue, 0, weights[0])])
    near = shifted(first, "grp", 1)
    back = shifted(first, "grp", -1)
    second = applied(position, 1, first, [(near, 0, weights[1])])
    both = shifted(jnp.concatenate([near, second]), "grp", 1)
    second = applied(position, 3, second, [(back, 0, weights[1])])
    third = applied(position, 2, second, [(both, 0, weights[1]), (both, 1, weights[2])])
    last = shifted(jnp.concatenate([both[residue.shape[0] :], third]), "grp", 1)
    return applied(position, 3, third, [(last, 0, weights[2]), (last, 1, weights[3])])


def after(place, value):
    mark = shifted(value[0, :8, :128], "core", 1)[0, 0]
    return jnp.where(mark != mark, jnp.zeros_like(place), place)


def reduced_over_z(blocks):
    share = blocks.shape[1]
    half = share // 2
    rows = blocks.reshape(-1, blocks.shape[2])
    middle = 4 * share + half
    up = shifted(rows[3 * share : middle], "z", 2)
    down = shifted(rows[middle : 6 * share], "z", -2)
    far_up = jnp.concatenate([blocks[2, :half] + up[share:], blocks[2, half:]])
    far_down = jnp.concatenate([blocks[6, :half], blocks[6, half:] + down[:half]])
    arrived = [
        shifted(far_up, "z", 2),
        shifted(far_down, "z", -2),
        shifted(blocks[1] + up[:share], "z", 1),
        shifted(blocks[7] + down[half:], "z", -1),
    ]
    return functools.reduce(lambda a, b: a + b, arrived, blocks[0])


def on_device(right_side, solved_factor, solved_users, diag_inverse, coupling):
    sizes = tuple(lax.axis_size(a) for a in COL)
    x, z, core = (lax.axis_index(a) for a in COL)
    place = [core, z] + [(x + o) % sizes[0] for o in ring_order(sizes[0])]
    place = jnp.stack(place).astype(jnp.int32)
    position = lax.axis_index("grp").reshape(1).astype(jnp.int32)
    users, factor = in_hbm(solved_users), in_hbm(solved_factor)

    own, sent = product(place, 0, 3, users, factor, sizes)
    other = shifted(sent[0], "core", 1)
    sent, other = lax.optimization_barrier((sent, other))
    far = own[0] + other
    near = own[1:] + shifted(sent[1:], "core", 1)
    cut = far.shape[0] // 2
    up = shifted(far[:cut], "x", 1)
    down = shifted(far[cut:], "x", -1)
    own, sent = product(after(place, far), 3, 1, users, factor, sizes)
    mine = own[0]
    near, sent = lax.optimization_barrier((near, sent))
    home = mine + shifted(sent[0], "core", 1)
    up = shifted(jnp.concatenate([near[0, :cut] + up, near[0, cut:]]), "x", 1)
    down = shifted(jnp.concatenate([near[1, :cut], near[1, cut:] + down]), "x", -1)
    weights = hop_weights(diag_inverse, coupling)
    home, weights = lax.optimization_barrier((home, weights))
    along_z = home + up + down
    residue = right_side.T - reduced_over_z(along_z)
    return chain(position, residue, weights).T


def solution(mesh):
    torus = Mesh(mesh.devices.reshape(mesh.shape["grp"], 4, 8, 2), ("grp",) + COL)
    placed = (P("grp", COL), P("grp", COL), P(COL, None), P("grp", None), P("grp", None))
    return jax.shard_map(
        on_device, mesh=torus, in_specs=placed, out_specs=P("grp", COL), check_vma=False
    )
```

```python
import functools

import jax
import jax.numpy as jnp
from jax import lax
from jax.experimental import pallas as pl
from jax.experimental.pallas import tpu as pltpu
from jax.sharding import Mesh
from jax.sharding import PartitionSpec as P

COL = ("x", "z", "core")


def shifted(value, axis, by):
    peers = lax.axis_size(axis)
    return lax.ppermute(value, axis, [(i, (i + by) % peers) for i in range(peers)])


def in_pieces(value, axis, by):
    return [shifted(part, axis, by) for part in jnp.split(value, 2)]


def in_hbm(value):
    return pltpu.with_memory_space_constraint(value, pltpu.HBM)


def halves(value):
    high = value.astype(jnp.bfloat16)
    return high, (value - high.astype(jnp.float32)).astype(jnp.bfloat16)


def contract(left, right, left_dim, right_dim):
    dims = (((left_dim,), (right_dim,)), ((), ()))
    return lax.dot_general(left, right, dims, preferred_element_type=jnp.float32)


def three_pass(left, right, left_dim, right_dim):
    left_high, left_low = halves(left)
    right_high, right_low = halves(right)
    return contract(left_high, right_high, left_dim, right_dim) + (
        contract(left_high, right_low, left_dim, right_dim)
        + contract(left_low, right_high, left_dim, right_dim)
    )


def ring_order(peers):
    return sorted(range(peers), key=lambda o: (-min(o, peers - o), o))


def product_body(n_z, n_core, place, users, factor, far_own, own, far_sent, sent):
    items, rows = users.shape[1], factor.shape[0]
    share = items // (n_z * n_core)
    total = three_pass(users[...], factor[...], 0, 1).reshape(n_z, n_core, share, rows)

    def keep(mine, kept, given):
        for k in range(n_z):
            ahead = lax.rem(k - place[1] + n_z, n_z)
            kept[ahead] = total[k, mine]
            given[ahead] = total[k, 1 - mine]

    for mine in range(2):
        for first in (True, False):
            kept, given = (far_own, far_sent) if first else (own.at[0], sent.at[0])
            chosen = (place[0] == mine) & ((pl.program_id(0) == 0) == first)
            pl.when(chosen)(functools.partial(keep, mine, kept, given))


def product(place, users, factor, sizes):
    n_x, n_z, n_core = sizes
    depth, items = users.shape
    rows = factor.shape[0]
    chunk, share = items // n_x, items // (n_x * n_z * n_core)
    specs = [
        pl.BlockSpec((n_z, share, rows), lambda i, s: (0, 0, 0)),
        pl.BlockSpec((1, n_z, share, rows), lambda i, s: (lax.max(i - 1, 0), 0, 0, 0)),
    ]
    shapes = [
        jax.ShapeDtypeStruct((n_z, share, rows), jnp.float32),
        jax.ShapeDtypeStruct((n_x - 1, n_z, share, rows), jnp.float32),
    ]
    return pl.pallas_call(
        functools.partial(product_body, n_z, n_core),
        grid_spec=pltpu.PrefetchScalarGridSpec(
            num_scalar_prefetch=1,
            grid=(n_x,),
            in_specs=[
                pl.BlockSpec((depth, chunk), lambda i, s: (0, s[2 + i])),
                pl.BlockSpec((rows, depth), lambda i, s: (0, 0)),
            ],
            out_specs=specs * 2,
        ),
        out_shape=shapes * 2,
        cost_estimate=pl.CostEstimate(
            flops=6 * items * rows * depth,
            transcendentals=0,
            bytes_accessed=4 * (items + rows) * depth + 4 * items * rows,
        ),
        compiler_params=pltpu.CompilerParams(vmem_limit_bytes=24 << 20),
    )(place, users, factor)


def weights_body(diag, coupling, *outs):
    block = diag.shape[0]
    outs[0][...], outs[1][...] = halves(diag[...].T)
    for h in range(coupling.shape[1] // block):
        value = -three_pass(coupling[:, h * block : (h + 1) * block], diag[...], 0, 1)
        outs[2 + 2 * h][...], outs[3 + 2 * h][...] = halves(value)


def hop_weights(diag, coupling):
    block = diag.shape[0]
    count = 1 + coupling.shape[1] // block
    outs = pl.pallas_call(
        weights_body,
        out_shape=[jax.ShapeDtypeStruct((block, block), jnp.bfloat16)] * (2 * count),
        cost_estimate=pl.CostEstimate(
            flops=6 * (count - 1) * block**3, transcendentals=0, bytes_accessed=8 * count * block**2
        ),
        compiler_params=pltpu.CompilerParams(vmem_limit_bytes=24 << 20),
    )(diag, coupling)
    return [tuple(outs[2 * k : 2 * k + 2]) for k in range(count)]


def apply_body(wanted, place, *refs):
    *values, base, high, low, out = refs
    total = jnp.zeros_like(base)
    for group, value in zip(wanted, values):
        total = total + (value[...] if group is None else jnp.where(place[0] == group, value[...], 0.0))
    value_high, value_low = halves(total)
    count = value_high.shape[0]
    both = contract(jnp.concatenate([value_high, value_low]), high[...], 1, 0)
    out[...] = base[...] + (both[:count] + both[count:] + contract(value_high, low[...], 1, 0))


def applied(position, base, values, weight):
    def whole(shape):
        return pl.BlockSpec(shape, lambda i, s: (0, 0))

    return pl.pallas_call(
        functools.partial(apply_body, [group for group, _ in values]),
        grid_spec=pltpu.PrefetchScalarGridSpec(
            num_scalar_prefetch=1,
            grid=(1,),
            in_specs=[whole(base.shape)] * (len(values) + 1) + [whole(half.shape) for half in weight],
            out_specs=whole(base.shape),
        ),
        out_shape=jax.ShapeDtypeStruct(base.shape, jnp.float32),
        compiler_params=pltpu.CompilerParams(vmem_limit_bytes=8 << 20),
    )(position, *[value for _, value in values], base, *weight)


def chain(position, residue, weights):
    groups = lax.axis_size("grp")
    result = applied(position, jnp.zeros_like(residue), [(None, residue)], weights[0])
    later = []
    for step in range(groups - 1):
        near = shifted(result, "grp", 1)
        far = [(step + by, shifted(result, "grp", by)) for by in range(2, groups - step)]
        if later:
            result = applied(position, result, later, weights[step])
        result = applied(position, result, [(step + 1, near)], weights[step + 1])
        later = far
    return result


def reduced_over_z(blocks):
    share = blocks.shape[1]
    half = share // 2
    rows = blocks.reshape(-1, blocks.shape[2])
    middle = 4 * share + half
    up = shifted(rows[3 * share : middle], "z", 2)
    down = shifted(rows[middle : 6 * share], "z", -2)
    far_up = jnp.concatenate([blocks[2, :half] + up[share:], blocks[2, half:]])
    far_down = jnp.concatenate([blocks[6, :half], blocks[6, half:] + down[:half]])
    arrived = [
        shifted(far_up, "z", 2),
        shifted(far_down, "z", -2),
        shifted(blocks[1] + up[:share], "z", 1),
        shifted(blocks[7] + down[half:], "z", -1),
    ]
    return functools.reduce(lambda a, b: a + b, arrived, blocks[0])


def on_device(right_side, solved_factor, solved_users, diag_inverse, coupling):
    sizes = tuple(lax.axis_size(a) for a in COL)
    x, z, core = (lax.axis_index(a) for a in COL)
    place = [core, z] + [(x + o) % sizes[0] for o in ring_order(sizes[0])]
    place = jnp.stack(place).astype(jnp.int32)
    position = lax.axis_index("grp").reshape(1).astype(jnp.int32)
    users, factor = in_hbm(solved_users), in_hbm(solved_factor)

    far_own, own, far_sent, sent = product(place, users, factor, sizes)
    other = shifted(far_sent, "core", 1)
    sent, other = lax.optimization_barrier((sent, other))
    far = in_pieces(far_own + other, "x", 2)
    near = own + shifted(sent, "core", 1)
    up = in_pieces(near[0], "x", 1)
    down = in_pieces(near[1], "x", -1)
    weights = hop_weights(diag_inverse, coupling)
    home, weights = lax.optimization_barrier((near[2], weights))
    along_z = jnp.concatenate([part + f + u + d for part, f, u, d in zip(jnp.split(home, 2), far, up, down)])
    residue = right_side.T - reduced_over_z(along_z)
    return chain(position, residue, weights).T


def solution(mesh):
    torus = Mesh(mesh.devices.reshape(mesh.shape["grp"], 4, 8, 2), ("grp",) + COL)
    placed = (P("grp", COL), P("grp", COL), P(COL, None), P("grp", None), P("grp", None))
    return jax.shard_map(
        on_device, mesh=torus, in_specs=placed, out_specs=P("grp", COL), check_vma=False
    )
```

```python
import functools

import jax
import jax.numpy as jnp
from jax import lax
from jax.experimental import pallas as pl
from jax.experimental.pallas import tpu as pltpu
from jax.sharding import Mesh
from jax.sharding import PartitionSpec as P

COL = ("x", "z", "core")


def shifted(value, axis, by):
    peers = lax.axis_size(axis)
    return lax.ppermute(value, axis, [(i, (i + by) % peers) for i in range(peers)])


def in_hbm(value):
    return pltpu.with_memory_space_constraint(value, pltpu.HBM)


def halves(value):
    high = value.astype(jnp.bfloat16)
    return high, (value - high.astype(jnp.float32)).astype(jnp.bfloat16)


def contract(left, right, left_dim, right_dim):
    dims = (((left_dim,), (right_dim,)), ((), ()))
    return lax.dot_general(left, right, dims, preferred_element_type=jnp.float32)


def three_pass(left, right, left_dim, right_dim):
    left_high, left_low = halves(left)
    right_high, right_low = halves(right)
    return contract(left_high, right_high, left_dim, right_dim) + (
        contract(left_high, right_low, left_dim, right_dim)
        + contract(left_low, right_high, left_dim, right_dim)
    )


def ring_order(peers):
    return sorted(range(peers), key=lambda o: (-min(o, peers - o), o))


def product_body(n_z, n_core, place, users, factor, far_own, own, far_sent, sent):
    items, rows = users.shape[1], factor.shape[0]
    share = items // (n_z * n_core)
    total = three_pass(users[...], factor[...], 0, 1).reshape(n_z, n_core, share, rows)

    def keep(mine, kept, given):
        for k in range(n_z):
            ahead = lax.rem(k - place[1] + n_z, n_z)
            kept[ahead] = total[k, mine]
            given[ahead] = total[k, 1 - mine]

    for mine in range(2):
        for first in (True, False):
            kept, given = (far_own, far_sent) if first else (own.at[0], sent.at[0])
            chosen = (place[0] == mine) & ((pl.program_id(0) == 0) == first)
            pl.when(chosen)(functools.partial(keep, mine, kept, given))


def product(place, users, factor, sizes):
    n_x, n_z, n_core = sizes
    depth, items = users.shape
    rows = factor.shape[0]
    chunk, share = items // n_x, items // (n_x * n_z * n_core)
    specs = [
        pl.BlockSpec((n_z, share, rows), lambda i, s: (0, 0, 0)),
        pl.BlockSpec((1, n_z, share, rows), lambda i, s: (lax.max(i - 1, 0), 0, 0, 0)),
    ]
    shapes = [
        jax.ShapeDtypeStruct((n_z, share, rows), jnp.float32),
        jax.ShapeDtypeStruct((n_x - 1, n_z, share, rows), jnp.float32),
    ]
    return pl.pallas_call(
        functools.partial(product_body, n_z, n_core),
        grid_spec=pltpu.PrefetchScalarGridSpec(
            num_scalar_prefetch=1,
            grid=(n_x,),
            in_specs=[
                pl.BlockSpec((depth, chunk), lambda i, s: (0, s[2 + i])),
                pl.BlockSpec((rows, depth), lambda i, s: (0, 0)),
            ],
            out_specs=specs * 2,
        ),
        out_shape=shapes * 2,
        cost_estimate=pl.CostEstimate(
            flops=6 * items * rows * depth,
            transcendentals=0,
            bytes_accessed=4 * (items + rows) * depth + 4 * items * rows,
        ),
        compiler_params=pltpu.CompilerParams(vmem_limit_bytes=24 << 20),
    )(place, users, factor)


def weights_body(diag, coupling, high, low):
    step = pl.program_id(0)

    def keep(value):
        high[0], low[0] = halves(value)

    pl.when(step == 0)(lambda: keep(diag[...].T))
    pl.when(step > 0)(lambda: keep(-three_pass(coupling[...], diag[...], 0, 1)))


def hop_weights(diag, coupling):
    block = diag.shape[0]
    count = 1 + coupling.shape[1] // block
    shape = jax.ShapeDtypeStruct((count, block, block), jnp.bfloat16)
    return pl.pallas_call(
        weights_body,
        grid=(count,),
        in_specs=[
            pl.BlockSpec((block, block), lambda i: (0, 0)),
            pl.BlockSpec((block, block), lambda i: (0, lax.max(i - 1, 0))),
        ],
        out_specs=[pl.BlockSpec((1, block, block), lambda i: (i, 0, 0))] * 2,
        out_shape=[shape] * 2,
        cost_estimate=pl.CostEstimate(
            flops=6 * (count - 1) * block**3, transcendentals=0, bytes_accessed=8 * count * block**2
        ),
        compiler_params=pltpu.CompilerParams(vmem_limit_bytes=24 << 20),
    )(diag, coupling)


def apply_body(wanted, place, *refs):
    *values, base, high, low, out = refs
    total = jnp.zeros_like(base)
    for group, value in zip(wanted, values):
        total = total + (value[...] if group is None else jnp.where(place[0] == group, value[...], 0.0))
    value_high, value_low = halves(total)
    count = value_high.shape[0]
    both = contract(jnp.concatenate([value_high, value_low]), high[0], 1, 0)
    out[...] = base[...] + (both[:count] + both[count:] + contract(value_high, low[0], 1, 0))


def applied(position, base, values, weights, index):
    whole = pl.BlockSpec(base.shape, lambda i, s: (0, 0))
    block = weights[0].shape[1]
    weight = pl.BlockSpec((1, block, block), lambda i, s: (index, 0, 0))
    return pl.pallas_call(
        functools.partial(apply_body, [group for group, _ in values]),
        grid_spec=pltpu.PrefetchScalarGridSpec(
            num_scalar_prefetch=1,
            grid=(1,),
            in_specs=[whole] * (len(values) + 1) + [weight] * 2,
            out_specs=whole,
        ),
        out_shape=jax.ShapeDtypeStruct(base.shape, jnp.float32),
        compiler_params=pltpu.CompilerParams(vmem_limit_bytes=8 << 20),
    )(position, *[value for _, value in values], base, *weights)


def chain(position, residue, weights):
    groups = lax.axis_size("grp")
    result = applied(position, jnp.zeros_like(residue), [(None, residue)], weights, 0)
    later = []
    for step in range(groups - 1):
        near = shifted(result, "grp", 1)
        far = [(step + by, shifted(result, "grp", by)) for by in range(2, groups - step)]
        if later:
            result = applied(position, result, later, weights, step)
        result = applied(position, result, [(step + 1, near)], weights, step + 1)
        later = far
    return result


def reduced_over_z(blocks):
    share = blocks.shape[1]
    half = share // 2
    rows = blocks.reshape(-1, blocks.shape[2])
    middle = 4 * share + half
    up = shifted(rows[3 * share : middle], "z", 2)
    down = shifted(rows[middle : 6 * share], "z", -2)
    far_up = jnp.concatenate([blocks[2, :half] + up[share:], blocks[2, half:]])
    far_down = jnp.concatenate([blocks[6, :half], blocks[6, half:] + down[:half]])
    arrived = [
        shifted(far_up, "z", 2),
        shifted(far_down, "z", -2),
        shifted(blocks[1] + up[:share], "z", 1),
        shifted(blocks[7] + down[half:], "z", -1),
    ]
    return functools.reduce(lambda a, b: a + b, arrived, blocks[0])


def on_device(right_side, solved_factor, solved_users, diag_inverse, coupling):
    sizes = tuple(lax.axis_size(a) for a in COL)
    x, z, core = (lax.axis_index(a) for a in COL)
    place = [core, z] + [(x + o) % sizes[0] for o in ring_order(sizes[0])]
    place = jnp.stack(place).astype(jnp.int32)
    position = lax.axis_index("grp").reshape(1).astype(jnp.int32)
    users, factor = in_hbm(solved_users), in_hbm(solved_factor)

    far_own, own, far_sent, sent = product(place, users, factor, sizes)
    far_other = shifted(far_sent, "core", 1)
    sent, far_other = lax.optimization_barrier((sent, far_other))
    far = far_own + far_other
    near = own + shifted(sent, "core", 1)
    cut = far.shape[0] // 2
    up = shifted(far[:cut], "x", 1)
    down = shifted(far[cut:], "x", -1)
    ups = [shifted(half, "x", 1) for half in (near[0, :cut] + up, near[0, cut:])]
    downs = [shifted(half, "x", -1) for half in (near[1, :cut], near[1, cut:] + down)]
    weights = hop_weights(diag_inverse, coupling)
    home, weights = lax.optimization_barrier((near[2], weights))
    sums = [home[:cut] + ups[0] + downs[0], home[cut:] + ups[1] + downs[1]]
    along_z = jnp.concatenate(sums)
    residue = right_side.T - reduced_over_z(along_z)
    return chain(position, residue, weights).T


def solution(mesh):
    torus = Mesh(mesh.devices.reshape(mesh.shape["grp"], 4, 8, 2), ("grp",) + COL)
    placed = (P("grp", COL), P("grp", COL), P(COL, None), P("grp", None), P("grp", None))
    return jax.shard_map(
        on_device, mesh=torus, in_specs=placed, out_specs=P("grp", COL), check_vma=False
    )
```

```python
import functools

import jax
import jax.numpy as jnp
from jax import lax
from jax.experimental import pallas as pl
from jax.experimental.pallas import tpu as pltpu
from jax.sharding import Mesh
from jax.sharding import PartitionSpec as P

COL = ("x", "z", "core")


def shifted(value, axis, by):
    peers = lax.axis_size(axis)
    return lax.ppermute(value, axis, [(i, (i + by) % peers) for i in range(peers)])


def in_pieces(value, axis, by):
    return jnp.concatenate([shifted(part, axis, by) for part in jnp.split(value, 2)])


def in_hbm(value):
    return pltpu.with_memory_space_constraint(value, pltpu.HBM)


def halves(value):
    high = value.astype(jnp.bfloat16)
    return high, (value - high.astype(jnp.float32)).astype(jnp.bfloat16)


def contract(left, right, left_dim, right_dim):
    dims = (((left_dim,), (right_dim,)), ((), ()))
    return lax.dot_general(left, right, dims, preferred_element_type=jnp.float32)


def three_pass(left, right, left_dim, right_dim):
    left_high, left_low = halves(left)
    right_high, right_low = halves(right)
    return contract(left_high, right_high, left_dim, right_dim) + (
        contract(left_high, right_low, left_dim, right_dim)
        + contract(left_low, right_high, left_dim, right_dim)
    )


def ring_order(peers):
    return sorted(range(peers), key=lambda o: (-min(o, peers - o), o))


def product_body(n_z, n_core, place, users, factor, far_own, own, far_sent, sent):
    items, rows = users.shape[1], factor.shape[0]
    share = items // (n_z * n_core)
    total = three_pass(users[...], factor[...], 0, 1).reshape(n_z, n_core, share, rows)

    def keep(mine, kept, given):
        for k in range(n_z):
            ahead = lax.rem(k - place[1] + n_z, n_z)
            kept[ahead] = total[k, mine]
            given[ahead] = total[k, 1 - mine]

    for mine in range(2):
        for first in (True, False):
            kept, given = (far_own, far_sent) if first else (own.at[0], sent.at[0])
            chosen = (place[0] == mine) & ((pl.program_id(0) == 0) == first)
            pl.when(chosen)(functools.partial(keep, mine, kept, given))


def product(place, users, factor, sizes):
    n_x, n_z, n_core = sizes
    depth, items = users.shape
    rows = factor.shape[0]
    chunk, share = items // n_x, items // (n_x * n_z * n_core)
    specs = [
        pl.BlockSpec((n_z, share, rows), lambda i, s: (0, 0, 0)),
        pl.BlockSpec((1, n_z, share, rows), lambda i, s: (lax.max(i - 1, 0), 0, 0, 0)),
    ]
    shapes = [
        jax.ShapeDtypeStruct((n_z, share, rows), jnp.float32),
        jax.ShapeDtypeStruct((n_x - 1, n_z, share, rows), jnp.float32),
    ]
    return pl.pallas_call(
        functools.partial(product_body, n_z, n_core),
        grid_spec=pltpu.PrefetchScalarGridSpec(
            num_scalar_prefetch=1,
            grid=(n_x,),
            in_specs=[
                pl.BlockSpec((depth, chunk), lambda i, s: (0, s[2 + i])),
                pl.BlockSpec((rows, depth), lambda i, s: (0, 0)),
            ],
            out_specs=specs * 2,
        ),
        out_shape=shapes * 2,
        cost_estimate=pl.CostEstimate(
            flops=6 * items * rows * depth,
            transcendentals=0,
            bytes_accessed=4 * (items + rows) * depth + 4 * items * rows,
        ),
        compiler_params=pltpu.CompilerParams(vmem_limit_bytes=24 << 20),
    )(place, users, factor)


def weights_body(diag, coupling, high, low):
    step = pl.program_id(0)

    def keep(value):
        high[0], low[0] = halves(value)

    pl.when(step == 0)(lambda: keep(diag[...].T))
    pl.when(step > 0)(lambda: keep(-three_pass(coupling[...], diag[...], 0, 1)))


def hop_weights(diag, coupling):
    block = diag.shape[0]
    count = 1 + coupling.shape[1] // block
    shape = jax.ShapeDtypeStruct((count, block, block), jnp.bfloat16)
    return pl.pallas_call(
        weights_body,
        grid=(count,),
        in_specs=[
            pl.BlockSpec((block, block), lambda i: (0, 0)),
            pl.BlockSpec((block, block), lambda i: (0, lax.max(i - 1, 0))),
        ],
        out_specs=[pl.BlockSpec((1, block, block), lambda i: (i, 0, 0))] * 2,
        out_shape=[shape] * 2,
        cost_estimate=pl.CostEstimate(
            flops=6 * (count - 1) * block**3, transcendentals=0, bytes_accessed=8 * count * block**2
        ),
        compiler_params=pltpu.CompilerParams(vmem_limit_bytes=24 << 20),
    )(diag, coupling)


def apply_body(wanted, place, *refs):
    *values, base, high, low, out = refs
    total = jnp.zeros_like(base)
    for group, value in zip(wanted, values):
        total = total + (value[...] if group is None else jnp.where(place[0] == group, value[...], 0.0))
    value_high, value_low = halves(total)
    count = value_high.shape[0]
    both = contract(jnp.concatenate([value_high, value_low]), high[0], 1, 0)
    out[...] = base[...] + (both[:count] + both[count:] + contract(value_high, low[0], 1, 0))


def applied(position, base, values, weights, index):
    whole = pl.BlockSpec(base.shape, lambda i, s: (0, 0))
    block = weights[0].shape[1]
    weight = pl.BlockSpec((1, block, block), lambda i, s: (index, 0, 0))
    return pl.pallas_call(
        functools.partial(apply_body, [group for group, _ in values]),
        grid_spec=pltpu.PrefetchScalarGridSpec(
            num_scalar_prefetch=1,
            grid=(1,),
            in_specs=[whole] * (len(values) + 1) + [weight] * 2,
            out_specs=whole,
        ),
        out_shape=jax.ShapeDtypeStruct(base.shape, jnp.float32),
        compiler_params=pltpu.CompilerParams(vmem_limit_bytes=8 << 20),
    )(position, *[value for _, value in values], base, *weights)


def chain(position, residue, weights):
    groups = lax.axis_size("grp")
    result = applied(position, jnp.zeros_like(residue), [(None, residue)], weights, 0)
    later = []
    for step in range(groups - 1):
        near = shifted(result, "grp", 1)
        far = [(step + by, shifted(result, "grp", by)) for by in range(2, groups - step)]
        if later:
            result = applied(position, result, later, weights, step)
        result = applied(position, result, [(step + 1, near)], weights, step + 1)
        later = far
    return result


def reduced_over_z(blocks):
    share = blocks.shape[1]
    half = share // 2
    rows = blocks.reshape(-1, blocks.shape[2])
    middle = 4 * share + half
    up = shifted(rows[3 * share : middle], "z", 2)
    down = shifted(rows[middle : 6 * share], "z", -2)
    far_up = jnp.concatenate([blocks[2, :half] + up[share:], blocks[2, half:]])
    far_down = jnp.concatenate([blocks[6, :half], blocks[6, half:] + down[:half]])
    arrived = [
        shifted(far_up, "z", 2),
        shifted(far_down, "z", -2),
        shifted(blocks[1] + up[:share], "z", 1),
        shifted(blocks[7] + down[half:], "z", -1),
    ]
    return functools.reduce(lambda a, b: a + b, arrived, blocks[0])


def on_device(right_side, solved_factor, solved_users, diag_inverse, coupling):
    sizes = tuple(lax.axis_size(a) for a in COL)
    x, z, core = (lax.axis_index(a) for a in COL)
    place = [core, z] + [(x + o) % sizes[0] for o in ring_order(sizes[0])]
    place = jnp.stack(place).astype(jnp.int32)
    position = lax.axis_index("grp").reshape(1).astype(jnp.int32)
    users, factor = in_hbm(solved_users), in_hbm(solved_factor)

    far_own, own, far_sent, sent = product(place, users, factor, sizes)
    far_other = shifted(far_sent, "core", 1)
    sent, far_other = lax.optimization_barrier((sent, far_other))
    far = far_own + far_other
    near = own + shifted(sent, "core", 1)
    cut = far.shape[0] // 2
    up = in_pieces(far[:cut], "x", 1)
    down = in_pieces(far[cut:], "x", -1)
    ups = [shifted(half, "x", 1) for half in (near[0, :cut] + up, near[0, cut:])]
    downs = [shifted(half, "x", -1) for half in (near[1, :cut], near[1, cut:] + down)]
    weights = hop_weights(diag_inverse, coupling)
    home, weights = lax.optimization_barrier((near[2], weights))
    sums = [home[:cut] + ups[0] + downs[0], home[cut:] + ups[1] + downs[1]]
    along_z = jnp.concatenate(sums)
    residue = right_side.T - reduced_over_z(along_z)
    return chain(position, residue, weights).T


def solution(mesh):
    torus = Mesh(mesh.devices.reshape(mesh.shape["grp"], 4, 8, 2), ("grp",) + COL)
    placed = (P("grp", COL), P("grp", COL), P(COL, None), P("grp", None), P("grp", None))
    return jax.shard_map(
        on_device, mesh=torus, in_specs=placed, out_specs=P("grp", COL), check_vma=False
    )
```

```python
import functools

import jax
import jax.numpy as jnp
from jax import lax
from jax.experimental import pallas as pl
from jax.experimental.pallas import tpu as pltpu
from jax.sharding import Mesh
from jax.sharding import PartitionSpec as P

COL = ("x", "z", "core")


def shifted(value, axis, by):
    peers = lax.axis_size(axis)
    return lax.ppermute(value, axis, [(i, (i + by) % peers) for i in range(peers)])


def in_hbm(value):
    return pltpu.with_memory_space_constraint(value, pltpu.HBM)


def halves(value):
    high = value.astype(jnp.bfloat16)
    return high, (value - high.astype(jnp.float32)).astype(jnp.bfloat16)


def contract(left, right, left_dim, right_dim):
    dims = (((left_dim,), (right_dim,)), ((), ()))
    return lax.dot_general(left, right, dims, preferred_element_type=jnp.float32)


def three_pass(left, right, left_dim, right_dim):
    left_high, left_low = halves(left)
    right_high, right_low = halves(right)
    return contract(left_high, right_high, left_dim, right_dim) + (
        contract(left_high, right_low, left_dim, right_dim)
        + contract(left_low, right_high, left_dim, right_dim)
    )


def ring_order(peers):
    return sorted(range(peers), key=lambda o: (-min(o, peers - o), o))


def product_body(n_z, n_core, place, users, factor, far_own, own, far_sent, sent):
    items, rows = users.shape[1], factor.shape[0]
    share = items // (n_z * n_core)
    total = three_pass(users[...], factor[...], 0, 1).reshape(n_z, n_core, share, rows)

    def keep(mine, kept, given):
        for k in range(n_z):
            ahead = lax.rem(k - place[1] + n_z, n_z)
            kept[ahead] = total[k, mine]
            given[ahead] = total[k, 1 - mine]

    for mine in range(2):
        for first in (True, False):
            kept, given = (far_own, far_sent) if first else (own.at[0], sent.at[0])
            chosen = (place[0] == mine) & ((pl.program_id(0) == 0) == first)
            pl.when(chosen)(functools.partial(keep, mine, kept, given))


def product(place, users, factor, sizes):
    n_x, n_z, n_core = sizes
    depth, items = users.shape
    rows = factor.shape[0]
    chunk, share = items // n_x, items // (n_x * n_z * n_core)
    specs = [
        pl.BlockSpec((n_z, share, rows), lambda i, s: (0, 0, 0)),
        pl.BlockSpec((1, n_z, share, rows), lambda i, s: (lax.max(i - 1, 0), 0, 0, 0)),
    ]
    shapes = [
        jax.ShapeDtypeStruct((n_z, share, rows), jnp.float32),
        jax.ShapeDtypeStruct((n_x - 1, n_z, share, rows), jnp.float32),
    ]
    return pl.pallas_call(
        functools.partial(product_body, n_z, n_core),
        grid_spec=pltpu.PrefetchScalarGridSpec(
            num_scalar_prefetch=1,
            grid=(n_x,),
            in_specs=[
                pl.BlockSpec((depth, chunk), lambda i, s: (0, s[2 + i])),
                pl.BlockSpec((rows, depth), lambda i, s: (0, 0)),
            ],
            out_specs=specs * 2,
        ),
        out_shape=shapes * 2,
        cost_estimate=pl.CostEstimate(
            flops=6 * items * rows * depth,
            transcendentals=0,
            bytes_accessed=4 * (items + rows) * depth + 4 * items * rows,
        ),
        compiler_params=pltpu.CompilerParams(vmem_limit_bytes=24 << 20),
    )(place, users, factor)


def weights_body(diag, coupling, high, low):
    high[0], low[0] = halves(-three_pass(coupling[...], diag[...], 0, 1))


def hop_weights(diag, coupling):
    block = diag.shape[0]
    count = coupling.shape[1] // block
    shape = jax.ShapeDtypeStruct((count, block, block), jnp.bfloat16)
    return pl.pallas_call(
        weights_body,
        grid=(count,),
        in_specs=[
            pl.BlockSpec((block, block), lambda i: (0, 0)),
            pl.BlockSpec((block, block), lambda i: (0, i)),
        ],
        out_specs=[pl.BlockSpec((1, block, block), lambda i: (i, 0, 0))] * 2,
        out_shape=[shape] * 2,
        cost_estimate=pl.CostEstimate(
            flops=6 * count * block**3, transcendentals=0, bytes_accessed=8 * (count + 1) * block**2
        ),
        compiler_params=pltpu.CompilerParams(vmem_limit_bytes=24 << 20),
    )(diag, coupling)


def solved_alone_body(residue, diag, out):
    out[...] = three_pass(residue[...], diag[...], 1, 1)


def solved_alone(residue, diag):
    return pl.pallas_call(
        solved_alone_body,
        out_shape=jax.ShapeDtypeStruct(residue.shape, jnp.float32),
        compiler_params=pltpu.CompilerParams(vmem_limit_bytes=8 << 20),
    )(residue, diag)


def apply_body(wanted, place, *refs):
    *values, base, high, low, out = refs
    total = jnp.zeros_like(base)
    for group, value in zip(wanted, values):
        total = total + (value[...] if group is None else jnp.where(place[0] == group, value[...], 0.0))
    value_high, value_low = halves(total)
    count = value_high.shape[0]
    both = contract(jnp.concatenate([value_high, value_low]), high[0], 1, 0)
    out[...] = base[...] + (both[:count] + both[count:] + contract(value_high, low[0], 1, 0))


def applied(position, base, values, weights, index):
    whole = pl.BlockSpec(base.shape, lambda i, s: (0, 0))
    block = weights[0].shape[1]
    weight = pl.BlockSpec((1, block, block), lambda i, s: (index, 0, 0))
    return pl.pallas_call(
        functools.partial(apply_body, [group for group, _ in values]),
        grid_spec=pltpu.PrefetchScalarGridSpec(
            num_scalar_prefetch=1,
            grid=(1,),
            in_specs=[whole] * (len(values) + 1) + [weight] * 2,
            out_specs=whole,
        ),
        out_shape=jax.ShapeDtypeStruct(base.shape, jnp.float32),
        compiler_params=pltpu.CompilerParams(vmem_limit_bytes=8 << 20),
    )(position, *[value for _, value in values], base, *weights)


def chain(position, residue, diag, weights):
    groups = lax.axis_size("grp")
    result = solved_alone(residue, diag)
    later = []
    for step in range(groups - 1):
        near = shifted(result, "grp", 1)
        far = [(step + by, shifted(result, "grp", by)) for by in range(2, groups - step)]
        if later:
            result = applied(position, result, later, weights, step - 1)
        result = applied(position, result, [(step + 1, near)], weights, step)
        later = far
    return result


def reduced_over_z(blocks):
    share = blocks.shape[1]
    half = share // 2
    rows = blocks.reshape(-1, blocks.shape[2])
    middle = 4 * share + half
    up = shifted(rows[3 * share : middle], "z", 2)
    down = shifted(rows[middle : 6 * share], "z", -2)
    far_up = jnp.concatenate([blocks[2, :half] + up[share:], blocks[2, half:]])
    far_down = jnp.concatenate([blocks[6, :half], blocks[6, half:] + down[:half]])
    arrived = [
        shifted(far_up, "z", 2),
        shifted(far_down, "z", -2),
        shifted(blocks[1] + up[:share], "z", 1),
        shifted(blocks[7] + down[half:], "z", -1),
    ]
    return functools.reduce(lambda a, b: a + b, arrived, blocks[0])


def on_device(right_side, solved_factor, solved_users, diag_inverse, coupling):
    sizes = tuple(lax.axis_size(a) for a in COL)
    x, z, core = (lax.axis_index(a) for a in COL)
    place = [core, z] + [(x + o) % sizes[0] for o in ring_order(sizes[0])]
    place = jnp.stack(place).astype(jnp.int32)
    position = lax.axis_index("grp").reshape(1).astype(jnp.int32)
    users, factor = in_hbm(solved_users), in_hbm(solved_factor)

    far_own, own, far_sent, sent = product(place, users, factor, sizes)
    far_other = shifted(far_sent, "core", 1)
    sent, far_other = lax.optimization_barrier((sent, far_other))
    far = far_own + far_other
    near = own + shifted(sent, "core", 1)
    cut = far.shape[0] // 2
    up = shifted(far[:cut], "x", 1)
    down = shifted(far[cut:], "x", -1)
    ups = [shifted(half, "x", 1) for half in (near[0, :cut] + up, near[0, cut:])]
    downs = [shifted(half, "x", -1) for half in (near[1, :cut], near[1, cut:] + down)]
    weights = hop_weights(diag_inverse, coupling)
    home, weights = lax.optimization_barrier((near[2], weights))
    sums = [home[:cut] + ups[0] + downs[0], home[cut:] + ups[1] + downs[1]]
    along_z = jnp.concatenate(sums)
    residue = right_side.T - reduced_over_z(along_z)
    return chain(position, residue, diag_inverse, weights).T


def solution(mesh):
    torus = Mesh(mesh.devices.reshape(mesh.shape["grp"], 4, 8, 2), ("grp",) + COL)
    placed = (P("grp", COL), P("grp", COL), P(COL, None), P("grp", None), P("grp", None))
    return jax.shard_map(
        on_device, mesh=torus, in_specs=placed, out_specs=P("grp", COL), check_vma=False
    )
```

```python
import functools

import jax
import jax.numpy as jnp
from jax import lax
from jax.experimental import pallas as pl
from jax.experimental.pallas import tpu as pltpu
from jax.sharding import Mesh
from jax.sharding import PartitionSpec as P

COL = ("x", "z", "core")


def shifted(value, axis, by):
    peers = lax.axis_size(axis)
    return lax.ppermute(value, axis, [(i, (i + by) % peers) for i in range(peers)])


def in_hbm(value):
    return pltpu.with_memory_space_constraint(value, pltpu.HBM)


def halves(value):
    high = value.astype(jnp.bfloat16)
    return high, (value - high.astype(jnp.float32)).astype(jnp.bfloat16)


def contract(left, right, left_dim, right_dim):
    dims = (((left_dim,), (right_dim,)), ((), ()))
    return lax.dot_general(left, right, dims, preferred_element_type=jnp.float32)


def three_pass(left, right, left_dim, right_dim):
    left_high, left_low = halves(left)
    right_high, right_low = halves(right)
    return contract(left_high, right_high, left_dim, right_dim) + (
        contract(left_high, right_low, left_dim, right_dim)
        + contract(left_low, right_high, left_dim, right_dim)
    )


def ring_order(peers):
    return sorted(range(peers), key=lambda o: (-min(o, peers - o), o))


def product_body(n_z, n_core, place, users, factor, far_own, own, far_sent, sent):
    items, rows = users.shape[1], factor.shape[0]
    share = items // (n_z * n_core)
    total = three_pass(users[...], factor[...], 0, 1).reshape(n_z, n_core, share, rows)

    def keep(mine, kept, given):
        for k in range(n_z):
            ahead = lax.rem(k - place[1] + 2 * n_z - 2, n_z)
            kept[ahead] = total[k, mine]
            given[ahead] = total[k, 1 - mine]

    for mine in range(2):
        for first in (True, False):
            kept, given = (far_own, far_sent) if first else (own.at[0], sent.at[0])
            chosen = (place[0] == mine) & ((pl.program_id(0) == 0) == first)
            pl.when(chosen)(functools.partial(keep, mine, kept, given))


def product(place, users, factor, sizes):
    n_x, n_z, n_core = sizes
    depth, items = users.shape
    rows = factor.shape[0]
    chunk, share = items // n_x, items // (n_x * n_z * n_core)
    specs = [
        pl.BlockSpec((n_z, share, rows), lambda i, s: (0, 0, 0)),
        pl.BlockSpec((1, n_z, share, rows), lambda i, s: (lax.max(i - 1, 0), 0, 0, 0)),
    ]
    shapes = [
        jax.ShapeDtypeStruct((n_z, share, rows), jnp.float32),
        jax.ShapeDtypeStruct((n_x - 1, n_z, share, rows), jnp.float32),
    ]
    return pl.pallas_call(
        functools.partial(product_body, n_z, n_core),
        grid_spec=pltpu.PrefetchScalarGridSpec(
            num_scalar_prefetch=1,
            grid=(n_x,),
            in_specs=[
                pl.BlockSpec((depth, chunk), lambda i, s: (0, s[2 + i])),
                pl.BlockSpec((rows, depth), lambda i, s: (0, 0)),
            ],
            out_specs=specs * 2,
        ),
        out_shape=shapes * 2,
        cost_estimate=pl.CostEstimate(
            flops=6 * items * rows * depth,
            transcendentals=0,
            bytes_accessed=4 * (items + rows) * depth + 4 * items * rows,
        ),
        compiler_params=pltpu.CompilerParams(vmem_limit_bytes=24 << 20),
    )(place, users, factor)


def weights_body(diag, coupling, high, low):
    high[0], low[0] = halves(-three_pass(coupling[...], diag[...], 0, 1))


def hop_weights(diag, coupling):
    block = diag.shape[0]
    count = coupling.shape[1] // block
    shape = jax.ShapeDtypeStruct((count, block, block), jnp.bfloat16)
    return pl.pallas_call(
        weights_body,
        grid=(count,),
        in_specs=[
            pl.BlockSpec((block, block), lambda i: (0, 0)),
            pl.BlockSpec((block, block), lambda i: (0, i)),
        ],
        out_specs=[pl.BlockSpec((1, block, block), lambda i: (i, 0, 0))] * 2,
        out_shape=[shape] * 2,
        cost_estimate=pl.CostEstimate(
            flops=6 * count * block**3, transcendentals=0, bytes_accessed=8 * (count + 1) * block**2
        ),
        compiler_params=pltpu.CompilerParams(vmem_limit_bytes=24 << 20),
    )(diag, coupling)


def solved_alone_body(residue, diag, out):
    out[...] = three_pass(residue[...], diag[...], 1, 1)


def solved_alone(residue, diag):
    return pl.pallas_call(
        solved_alone_body,
        out_shape=jax.ShapeDtypeStruct(residue.shape, jnp.float32),
        compiler_params=pltpu.CompilerParams(vmem_limit_bytes=8 << 20),
    )(residue, diag)


def apply_body(wanted, place, *refs):
    *values, base, high, low, out = refs
    total = jnp.zeros_like(base)
    for group, value in zip(wanted, values):
        total = total + (value[...] if group is None else jnp.where(place[0] == group, value[...], 0.0))
    value_high, value_low = halves(total)
    count = value_high.shape[0]
    both = contract(jnp.concatenate([value_high, value_low]), high[0], 1, 0)
    out[...] = base[...] + (both[:count] + both[count:] + contract(value_high, low[0], 1, 0))


def applied(position, base, values, weights, index):
    whole = pl.BlockSpec(base.shape, lambda i, s: (0, 0))
    block = weights[0].shape[1]
    weight = pl.BlockSpec((1, block, block), lambda i, s: (index, 0, 0))
    return pl.pallas_call(
        functools.partial(apply_body, [group for group, _ in values]),
        grid_spec=pltpu.PrefetchScalarGridSpec(
            num_scalar_prefetch=1,
            grid=(1,),
            in_specs=[whole] * (len(values) + 1) + [weight] * 2,
            out_specs=whole,
        ),
        out_shape=jax.ShapeDtypeStruct(base.shape, jnp.float32),
        compiler_params=pltpu.CompilerParams(vmem_limit_bytes=8 << 20),
    )(position, *[value for _, value in values], base, *weights)


def chain(position, residue, diag, weights):
    groups = lax.axis_size("grp")
    result = solved_alone(residue, diag)
    later = []
    for step in range(groups - 1):
        near = shifted(result, "grp", 1)
        far = [(step + by, shifted(result, "grp", by)) for by in range(2, groups - step)]
        if later:
            result = applied(position, result, later, weights, step - 1)
        result = applied(position, result, [(step + 1, near)], weights, step)
        later = far
    return result


def reduced_over_z(early, late):
    share, rows = early.shape[1:]
    half = share // 2
    far = early[1:].reshape(-1, rows)
    up = shifted(far[: share + half], "z", 2)
    down = shifted(far[share + half :], "z", -2)
    far_up = jnp.concatenate([early[0, :half] + up[share:], early[0, half:]])
    far_down = jnp.concatenate([late[0, :half], late[0, half:] + down[:half]])
    arrived = [
        shifted(far_up, "z", 2),
        shifted(far_down, "z", -2),
        shifted(late[3] + up[:share], "z", 1),
        shifted(late[1] + down[half:], "z", -1),
    ]
    return functools.reduce(lambda a, b: a + b, arrived, late[2])


def on_device(right_side, solved_factor, solved_users, diag_inverse, coupling):
    sizes = tuple(lax.axis_size(a) for a in COL)
    x, z, core = (lax.axis_index(a) for a in COL)
    place = [core, z] + [(x + o) % sizes[0] for o in ring_order(sizes[0])]
    place = jnp.stack(place).astype(jnp.int32)
    position = lax.axis_index("grp").reshape(1).astype(jnp.int32)
    users, factor = in_hbm(solved_users), in_hbm(solved_factor)

    far_own, own, far_sent, sent = product(place, users, factor, sizes)
    far_other = shifted(far_sent, "core", 1)
    sent, far_other = lax.optimization_barrier((sent, far_other))
    far = far_own + far_other
    near = own + shifted(sent, "core", 1)
    cut = far.shape[0] // 2
    up = shifted(far[:cut], "x", 1)
    down = shifted(far[cut:], "x", -1)
    ups = [shifted(half, "x", 1) for half in (near[0, :cut] + up, near[0, cut:])]
    downs = [shifted(half, "x", -1) for half in (near[1, :cut], near[1, cut:] + down)]
    weights = hop_weights(diag_inverse, coupling)
    home, weights = lax.optimization_barrier((near[2], weights))
    early = home[:cut] + ups[0] + downs[0]
    early, home = lax.optimization_barrier((early, home))
    late = home[cut:] + ups[1] + downs[1]
    residue = right_side.T - reduced_over_z(early, late)
    return chain(position, residue, diag_inverse, weights).T


def solution(mesh):
    torus = Mesh(mesh.devices.reshape(mesh.shape["grp"], 4, 8, 2), ("grp",) + COL)
    placed = (P("grp", COL), P("grp", COL), P(COL, None), P("grp", None), P("grp", None))
    return jax.shard_map(
        on_device, mesh=torus, in_specs=placed, out_specs=P("grp", COL), check_vma=False
    )
```

```python
import functools

import jax
import jax.numpy as jnp
from jax import lax
from jax.experimental import pallas as pl
from jax.experimental.pallas import tpu as pltpu
from jax.sharding import Mesh
from jax.sharding import PartitionSpec as P

COL = ("x", "z", "core")


def shifted(value, axis, by):
    peers = lax.axis_size(axis)
    return lax.ppermute(value, axis, [(i, (i + by) % peers) for i in range(peers)])


def in_hbm(value):
    return pltpu.with_memory_space_constraint(value, pltpu.HBM)


def halves(value):
    high = value.astype(jnp.bfloat16)
    return high, (value - high.astype(jnp.float32)).astype(jnp.bfloat16)


def contract(left, right, left_dim, right_dim):
    dims = (((left_dim,), (right_dim,)), ((), ()))
    return lax.dot_general(left, right, dims, preferred_element_type=jnp.float32)


def three_pass(left, right, left_dim, right_dim):
    left_high, left_low = halves(left)
    right_high, right_low = halves(right)
    return contract(left_high, right_high, left_dim, right_dim) + (
        contract(left_high, right_low, left_dim, right_dim)
        + contract(left_low, right_high, left_dim, right_dim)
    )


def ring_order(peers):
    return sorted(range(peers), key=lambda o: (-min(o, peers - o), o))


def product_body(n_z, n_core, place, users, factor, far_own, own, far_sent, sent):
    items, rows = users.shape[1], factor.shape[0]
    share = items // (n_z * n_core)
    total = three_pass(users[...], factor[...], 0, 1).reshape(n_z, n_core, share, rows)

    def keep(mine, kept, given):
        for k in range(n_z):
            ahead = lax.rem(k - place[1] + 2 * n_z - 2, n_z)
            kept[ahead] = total[k, mine]
            given[ahead] = total[k, 1 - mine]

    for mine in range(2):
        for first in (True, False):
            kept, given = (far_own, far_sent) if first else (own.at[0], sent.at[0])
            chosen = (place[0] == mine) & ((pl.program_id(0) == 0) == first)
            pl.when(chosen)(functools.partial(keep, mine, kept, given))


def product(place, users, factor, sizes):
    n_x, n_z, n_core = sizes
    depth, items = users.shape
    rows = factor.shape[0]
    chunk, share = items // n_x, items // (n_x * n_z * n_core)
    specs = [
        pl.BlockSpec((n_z, share, rows), lambda i, s: (0, 0, 0)),
        pl.BlockSpec((1, n_z, share, rows), lambda i, s: (lax.max(i - 1, 0), 0, 0, 0)),
    ]
    shapes = [
        jax.ShapeDtypeStruct((n_z, share, rows), jnp.float32),
        jax.ShapeDtypeStruct((n_x - 1, n_z, share, rows), jnp.float32),
    ]
    return pl.pallas_call(
        functools.partial(product_body, n_z, n_core),
        grid_spec=pltpu.PrefetchScalarGridSpec(
            num_scalar_prefetch=1,
            grid=(n_x,),
            in_specs=[
                pl.BlockSpec((depth, chunk), lambda i, s: (0, s[2 + i])),
                pl.BlockSpec((rows, depth), lambda i, s: (0, 0)),
            ],
            out_specs=specs * 2,
        ),
        out_shape=shapes * 2,
        cost_estimate=pl.CostEstimate(
            flops=6 * items * rows * depth,
            transcendentals=0,
            bytes_accessed=4 * (items + rows) * depth + 4 * items * rows,
        ),
        compiler_params=pltpu.CompilerParams(vmem_limit_bytes=24 << 20),
    )(place, users, factor)


def weights_body(diag, coupling, high, low):
    high[0], low[0] = halves(-three_pass(coupling[...], diag[...], 0, 1))


def hop_weights(diag, coupling):
    block = diag.shape[0]
    count = coupling.shape[1] // block
    shape = jax.ShapeDtypeStruct((count, block, block), jnp.bfloat16)
    return pl.pallas_call(
        weights_body,
        grid=(count,),
        in_specs=[
            pl.BlockSpec((block, block), lambda i: (0, 0)),
            pl.BlockSpec((block, block), lambda i: (0, i)),
        ],
        out_specs=[pl.BlockSpec((1, block, block), lambda i: (i, 0, 0))] * 2,
        out_shape=[shape] * 2,
        cost_estimate=pl.CostEstimate(
            flops=6 * count * block**3, transcendentals=0, bytes_accessed=8 * (count + 1) * block**2
        ),
        compiler_params=pltpu.CompilerParams(vmem_limit_bytes=24 << 20),
    )(diag, coupling)


def solved_alone_body(residue, diag, out):
    out[...] = three_pass(residue[...], diag[...], 1, 1)


def solved_alone(residue, diag):
    return pl.pallas_call(
        solved_alone_body,
        out_shape=jax.ShapeDtypeStruct(residue.shape, jnp.float32),
        compiler_params=pltpu.CompilerParams(vmem_limit_bytes=8 << 20),
    )(residue, diag)


def apply_body(wanted, place, *refs):
    *values, base, high, low, out = refs
    total = jnp.zeros_like(base)
    for group, value in zip(wanted, values):
        total = total + (value[...] if group is None else jnp.where(place[0] == group, value[...], 0.0))
    value_high, value_low = halves(total)
    count = value_high.shape[0]
    both = contract(jnp.concatenate([value_high, value_low]), high[0], 1, 0)
    out[...] = base[...] + (both[:count] + both[count:] + contract(value_high, low[0], 1, 0))


def applied(position, base, values, weights, index):
    whole = pl.BlockSpec(base.shape, lambda i, s: (0, 0))
    block = weights[0].shape[1]
    weight = pl.BlockSpec((1, block, block), lambda i, s: (index, 0, 0))
    return pl.pallas_call(
        functools.partial(apply_body, [group for group, _ in values]),
        grid_spec=pltpu.PrefetchScalarGridSpec(
            num_scalar_prefetch=1,
            grid=(1,),
            in_specs=[whole] * (len(values) + 1) + [weight] * 2,
            out_specs=whole,
        ),
        out_shape=jax.ShapeDtypeStruct(base.shape, jnp.float32),
        compiler_params=pltpu.CompilerParams(vmem_limit_bytes=8 << 20),
    )(position, *[value for _, value in values], base, *weights)


def chain(position, residue, diag, weights):
    groups = lax.axis_size("grp")
    result = solved_alone(residue, diag)
    later = []
    for step in range(groups - 1):
        near = shifted(result, "grp", 1)
        far = [(step + by, shifted(result, "grp", by)) for by in range(2, groups - step)]
        if later:
            result = applied(position, result, later, weights, step - 1)
        result = applied(position, result, [(step + 1, near)], weights, step)
        later = far
    return result


def reduced_over_z(early, late):
    share, rows = early.shape[1:]
    half = share // 2
    far = early[1:].reshape(-1, rows)
    up = shifted(far[: share + half], "z", 2)
    down = shifted(far[share + half :], "z", -2)
    far_up = jnp.concatenate([early[0, :half] + up[share:], early[0, half:]])
    far_down = jnp.concatenate([late[0, :half], late[0, half:] + down[:half]])
    arrived = [
        shifted(far_up, "z", 2),
        shifted(far_down, "z", -2),
        shifted(late[3] + up[:share], "z", 1),
        shifted(late[1] + down[half:], "z", -1),
    ]
    return functools.reduce(lambda a, b: a + b, arrived, late[2])


def on_device(right_side, solved_factor, solved_users, diag_inverse, coupling):
    sizes = tuple(lax.axis_size(a) for a in COL)
    x, z, core = (lax.axis_index(a) for a in COL)
    place = [core, z] + [(x + o) % sizes[0] for o in ring_order(sizes[0])]
    place = jnp.stack(place).astype(jnp.int32)
    position = lax.axis_index("grp").reshape(1).astype(jnp.int32)
    users, factor = in_hbm(solved_users), in_hbm(solved_factor)

    far_own, own, far_sent, sent = product(place, users, factor, sizes)
    far_other = shifted(far_sent, "core", 1)
    sent, far_other = lax.optimization_barrier((sent, far_other))
    far = far_own + far_other
    near = own + shifted(sent, "core", 1)
    cut = far.shape[0] // 2
    up = shifted(far[:cut], "x", 1)
    down = shifted(far[cut:], "x", -1)
    weights = hop_weights(diag_inverse, coupling)
    ahead, weights = lax.optimization_barrier((near[0], weights))
    ups = [shifted(half, "x", 1) for half in (ahead[:cut] + up, ahead[cut:])]
    downs = [shifted(half, "x", -1) for half in (near[1, :cut], near[1, cut:] + down)]
    home = near[2]
    early = home[:cut] + ups[0] + downs[0]
    early, home = lax.optimization_barrier((early, home))
    late = home[cut:] + ups[1] + downs[1]
    residue = right_side.T - reduced_over_z(early, late)
    return chain(position, residue, diag_inverse, weights).T


def solution(mesh):
    torus = Mesh(mesh.devices.reshape(mesh.shape["grp"], 4, 8, 2), ("grp",) + COL)
    placed = (P("grp", COL), P("grp", COL), P(COL, None), P("grp", None), P("grp", None))
    return jax.shard_map(
        on_device, mesh=torus, in_specs=placed, out_specs=P("grp", COL), check_vma=False
    )
```
